32 devices in a mesh: seq: 4 (over x, core), grp: 8 (over z, y).
Axes of the slice: x: 2, y: 2, z: 4, core: 2. Of those that a mesh axis runs over, the one named last changes fastest.
Arguments:
- conv_input: bfloat16 [8, 512, 2688], P('grp', 'seq'), may hold values from -6 to 6
- conv_weight: float32 [4, 2688], replicated, may hold values from -3 to 3
- step_raw: float32 [8, 512, 40], P('grp', 'seq'), may hold values from -9 to 6
- rate_log: float32 [40], replicated, may hold values from -3 to 3.1
- skip_gain: float32 [40], replicated, may hold values from 0.5 to 1.5
- gate_input: bfloat16 [8, 512, 2560], P('grp', 'seq'), may hold values from -6 to 6
- norm_gain: float32 [2560], replicated, may hold values from 0.1 to 1.9
- out_weight: bfloat16 [2560, 2560], P('grp'), may hold values from -0.125 to 0.125
- residual: bfloat16 [8, 512, 2560], P('grp', 'seq'), may hold values from -6 to 6
- moe_gain: float32 [2560], replicated, may hold values from 0.1 to 1.9
- w_gate: bfloat16 [8, 2560, 512], P('grp'), may hold values from -0.125 to 0.125
- w_up: bfloat16 [8, 2560, 512], P('grp'), may hold values from -0.125 to 0.125
- w_down: bfloat16 [8, 512, 2560], P('grp'), may hold values from -0.25 to 0.25
- routes: int32 [8, 512, 2], P('grp', 'seq'), may hold values from 0 to 7, as said below
- route_weights: float32 [8, 512, 2], P('grp', 'seq'), may hold values from 0.2 to 1
Outputs:
- layer_out: bfloat16 [8, 512, 2560], P('grp', 'seq')
The draws below stay inside these ranges and needn't reach their ends.
Inputs may be any that keep to these rules, and one draw needn't show every extreme that they name: `routes`: within the rows of one device (each aligned block of 128 frames of one manuscript) no expert is named by more than 64 entries, and one expert, the same in every block, is named by exactly 64; the two entries of a frame differ.
All inputs are finite; a program needn't handle non-finite values.
Results may differ from the reference program's by a relative error of at most 0.012.
Values may be sent and summed in bfloat16 or wider, within the bound.
A program may use at most 128 MiB of HBM per device.

```python
import math
import jax
import jax.numpy as jnp
from jax import lax

D = 2560
HEADS = 40
HEAD_DIM = 64
STATE = 64
CONV = 4
FF = 512
TOK_DEV = 128
INNER = 2560
CHANNELS = 2688
FRAMES = 512
MSS = 8
EXPERTS = 8
MOST = 64


def draw_routes(key, part):
    hot_key = jax.random.fold_in(key, 11)
    hot_expert = jax.random.randint(hot_key, (), 0, EXPERTS)
    block_total = MSS * (FRAMES // TOK_DEV)
    block_keys = jax.random.split(jax.random.fold_in(key, 12), block_total)

    def one_block(block_key):
        order_key, shuffle_key = jax.random.split(block_key)
        order = jax.random.permutation(order_key, (EXPERTS - 1) * MOST)
        others = order[:2 * TOK_DEV - MOST] // MOST
        others = others + (others >= hot_expert).astype(others.dtype)
        labels = jnp.sort(jnp.concatenate([jnp.full((MOST,), hot_expert, jnp.int32), others.astype(jnp.int32)]))
        pairs = jnp.stack([labels[:TOK_DEV], labels[TOK_DEV:]], axis=1)
        shuffle = jax.random.permutation(shuffle_key, TOK_DEV)
        return pairs[shuffle]
    blocks = jax.vmap(one_block)(block_keys)
    return blocks.reshape(MSS, FRAMES, 2).astype(jnp.int32)


def draw_step_raw(key, part):
    noise_key, offset_key, place_key = jax.random.split(jax.random.fold_in(key, 21), 3)
    random_jitter = 0.5 * jnp.clip(jax.random.normal(noise_key, (MSS, FRAMES, HEADS), jnp.float32), -3.0, 3.0)
    shift_amounts = jax.random.uniform(offset_key, (MSS, FRAMES // TOK_DEV, 1, HEADS), jnp.float32, -0.7, 0.7)
    shift_amounts = jnp.broadcast_to(shift_amounts, (MSS, FRAMES // TOK_DEV, TOK_DEV, HEADS)).reshape(MSS, FRAMES, HEADS)
    destination_slots = jax.random.randint(place_key, (MSS, 3), 0, FRAMES)
    page_frame_index = jnp.arange(FRAMES)
    spike_mask = jnp.any(page_frame_index[None, :, None] == destination_slots[:, None, :], axis=2).astype(jnp.float32)
    return (-6.0 + random_jitter + shift_amounts + 9.0 * spike_mask[:, :, None]).astype(jnp.float32)


def draw_rate_log(key, part):
    pick_key, slow_key, fast_key = jax.random.split(jax.random.fold_in(key, 31), 3)
    fast_heads = jax.random.uniform(pick_key, (HEADS,), jnp.float32) < 0.5
    slow_rates = jax.random.uniform(slow_key, (HEADS,), jnp.float32, math.log(0.06), math.log(0.15))
    fast_rates = jax.random.uniform(fast_key, (HEADS,), jnp.float32, math.log(8.0), math.log(20.0))
    return jnp.where(fast_heads, fast_rates, slow_rates).astype(jnp.float32)


def block_scale(key, extent, cuts, smallest, top_value):
    gain, own = 1.0, jax.random.fold_in(key, 6)
    for axis_at, parts in cuts:
        heights = jnp.exp(jax.random.uniform(jax.random.fold_in(own, axis_at), (parts,), jnp.float32, smallest / len(cuts), top_value / len(cuts)))
        gain = gain * jnp.repeat(heights, extent[axis_at] // parts).reshape([-1 if axis == axis_at else 1 for axis in range(len(extent))])
    return gain


def bell_draw(key, shape, spread, most, cuts=(), held_as=jnp.bfloat16):
    values = spread * jax.random.normal(key, shape, jnp.float32)
    if cuts:
        values = values * block_scale(key, shape, cuts, -0.22, 0.18)
    return jnp.clip(values, -most, most).astype(held_as)


def setup_inputs(seed: int = 0) -> dict:
    splits = jax.random.split(jax.random.key(seed), 16)
    return {
        "conv_input": bell_draw(splits[0], (MSS, FRAMES, CHANNELS), 1.0, 6.0, ((0, 8), (1, 4))),
        "conv_weight": bell_draw(splits[1], (CONV, CHANNELS), CONV ** -0.5, 3.0, (), jnp.float32),
        "step_raw": draw_step_raw(jax.random.fold_in(splits[15], 71), 0),
        "rate_log": draw_rate_log(jax.random.fold_in(splits[15], 71), 0),
        "skip_gain": jnp.clip(jax.random.uniform(splits[4], (HEADS,), jnp.float32, 0.5, 1.5), 0.5, 1.5),
        "gate_input": bell_draw(splits[5], (MSS, FRAMES, INNER), 1.0, 6.0, ((0, 8), (1, 4))),
        "norm_gain": jnp.clip(1.0 + 0.18 * jax.random.normal(splits[6], (INNER,), jnp.float32), 0.1, 1.9),
        "out_weight": bell_draw(splits[7], (INNER, D), INNER ** -0.5, 0.125, ((0, 8),)),
        "residual": bell_draw(splits[8], (MSS, FRAMES, D), 1.0, 6.0, ((0, 8), (1, 4))),
        "moe_gain": jnp.clip(1.0 + 0.18 * jax.random.normal(splits[9], (D,), jnp.float32), 0.1, 1.9),
        "w_gate": bell_draw(splits[10], (EXPERTS, D, FF), D ** -0.5, 0.125, ((0, 8),)),
        "w_up": bell_draw(splits[11], (EXPERTS, D, FF), D ** -0.5, 0.125, ((0, 8),)),
        "w_down": bell_draw(splits[12], (EXPERTS, FF, D), FF ** -0.5, 0.25, ((0, 8),)),
        "routes": draw_routes(jax.random.fold_in(splits[15], 71), 0),
        "route_weights": jnp.clip(0.2 + 0.8 * jax.random.uniform(splits[14], (MSS, FRAMES, 2), jnp.float32) ** block_scale(splits[14], (MSS, FRAMES, 2), ((0, 8), (1, 4)), -0.2, 0.2), 0.2, 1.0),
    }


EPSILON = 1e-05

def reference(conv_input, conv_weight, step_raw, rate_log, skip_gain, gate_input, norm_gain, out_weight, residual, moe_gain, w_gate, w_up, w_down, routes, route_weights):
    highest = lax.Precision.HIGHEST
    block_count = FRAMES // TOK_DEV

    def ssd_block(ssm_state, pieces):
        x_block, b_block, c_block, step_block, log_block = pieces
        length = x_block.shape[0]
        cumulative = jnp.cumsum(log_block, axis=0)
        x_values = x_block.astype(jnp.float32).reshape(length, HEADS, HEAD_DIM)
        b_values = b_block.astype(jnp.float32)
        c_values = c_block.astype(jnp.float32)
        scores = jnp.dot(c_block, b_block.T, preferred_element_type=jnp.float32)
        positions = jnp.arange(length, dtype=jnp.int32)
        causal = positions[:, None] >= positions[None, :]
        by_head = cumulative.T
        gap_log = by_head[:, :, None] - by_head[:, None, :]
        decay_mask = jnp.where(causal[None], jnp.exp(jnp.where(causal[None], gap_log, jnp.float32(0.0))), jnp.float32(0.0))
        mixing = scores[None] * decay_mask * step_block.T[:, None, :]
        within = jnp.einsum('hts,shp->thp', mixing, x_values, precision=highest)
        carried = jnp.einsum('tn,hpn->thp', c_values, ssm_state, precision=highest) * jnp.exp(cumulative)[:, :, None]
        tail_weight = jnp.exp(cumulative[-1][None, :] - cumulative) * step_block
        local_state = jnp.einsum('shp,sn->hpn', x_values * tail_weight[:, :, None], b_values, precision=highest)
        new_state = jnp.exp(cumulative[-1])[:, None, None] * ssm_state + local_state
        block_out = within + carried + skip_gain[None, :, None] * x_values
        return (new_state, block_out.reshape(length, HEADS * HEAD_DIM))

    def mixer(pieces):
        frames_in, raw_steps, gate_rows, residual_rows = pieces
        padded = jnp.concatenate([jnp.zeros((CONV - 1, CHANNELS), jnp.float32), frames_in.astype(jnp.float32)], axis=0)
        summed = conv_weight[0][None, :] * padded[0:FRAMES]
        for offset in range(1, CONV):
            summed = summed + conv_weight[offset][None, :] * padded[offset:offset + FRAMES]
        signal = jax.nn.silu(summed).astype(jnp.bfloat16)
        x_part = signal[:, :INNER]
        b_part = signal[:, INNER:INNER + STATE]
        c_part = signal[:, INNER + STATE:]
        step_size = jax.nn.softplus(raw_steps)
        log_decay = -step_size * jnp.exp(rate_log)[None, :]
        blocks = (x_part.reshape(block_count, TOK_DEV, INNER), b_part.reshape(block_count, TOK_DEV, STATE), c_part.reshape(block_count, TOK_DEV, STATE), step_size.reshape(block_count, TOK_DEV, HEADS), log_decay.reshape(block_count, TOK_DEV, HEADS))
        start_state = jnp.zeros((HEADS, HEAD_DIM, STATE), jnp.float32)
        final_state, outputs = lax.scan(ssd_block, start_state, blocks)
        ssd_out = outputs.reshape(FRAMES, INNER)
        gated_out = ssd_out * jax.nn.silu(gate_rows.astype(jnp.float32))
        mean_square = lax.optimization_barrier(jnp.mean(gated_out * gated_out, axis=1, keepdims=True))
        normed = (gated_out * lax.rsqrt(mean_square + EPSILON) * norm_gain[None, :]).astype(jnp.bfloat16)
        projected = jnp.dot(normed, out_weight, preferred_element_type=jnp.float32)
        return (residual_rows.astype(jnp.float32) + projected).astype(jnp.bfloat16)
    mixed_out = lax.map(mixer, (conv_input, step_raw, gate_input, residual))
    total_rows = MSS * FRAMES
    mixed_flat = mixed_out.reshape(total_rows, D).astype(jnp.float32)
    mean_square = lax.optimization_barrier(jnp.mean(mixed_flat * mixed_flat, axis=1, keepdims=True))
    moe_in = (mixed_flat * lax.rsqrt(mean_square + EPSILON) * moe_gain[None, :]).astype(jnp.bfloat16)
    assigned = routes.reshape(-1).astype(jnp.int32)
    token_of = (jnp.arange(2 * total_rows, dtype=jnp.int32) // 2).astype(jnp.int32)
    weight_of = route_weights.reshape(-1)
    capacity = MOST * MSS * (FRAMES // TOK_DEV)

    def per_expert(running, expert):
        order = jnp.argsort((assigned != expert).astype(jnp.int32), stable=True)[:capacity].astype(jnp.int32)
        valid = assigned[order] == expert
        picked = token_of[order]
        incoming_rows = moe_in[picked]
        gate_part = jnp.dot(incoming_rows, w_gate[expert], preferred_element_type=jnp.float32)
        up_part = jnp.dot(incoming_rows, w_up[expert], preferred_element_type=jnp.float32)
        expert_hidden = (jax.nn.silu(gate_part) * up_part).astype(jnp.bfloat16)
        expert_out = jnp.dot(expert_hidden, w_down[expert], preferred_element_type=jnp.float32).astype(jnp.bfloat16)
        scale = jnp.where(valid, weight_of[order], jnp.float32(0.0))
        running = running.at[picked].add(scale[:, None] * expert_out.astype(jnp.float32))
        return (running, None)
    total, unused = lax.scan(per_expert, mixed_flat, jnp.arange(EXPERTS, dtype=jnp.int32))
    return total.astype(jnp.bfloat16).reshape(MSS, FRAMES, D)
```

```python
import jax
import jax.numpy as jnp
from jax import lax
from jax.sharding import PartitionSpec as P

EPSILON = 1e-05


def from_behind(value, axis, steps):
    count = lax.axis_size(axis)
    first, last = (max(0, -steps), min(count, count - steps))
    return lax.ppermute(value, axis, [(source, source + steps) for source in range(first, last)])


def on_device(
    conv_input,
    conv_weight,
    step_raw,
    rate_log,
    skip_gain,
    gate_input,
    norm_gain,
    out_weight,
    residual,
    moe_gain,
    w_gate,
    w_up,
    w_down,
    routes,
    route_weights,
):
    half = jnp.bfloat16
    ring = lax.axis_size("seq")
    own = lax.axis_index("seq")
    share = out_weight.shape[1] // ring
    weight_share = lax.all_gather(
        lax.dynamic_slice_in_dim(out_weight, own * share, share, axis=1), "grp", axis=0, tiled=True
    )
    frames_in = conv_input[0]
    row_count = frames_in.shape[0]
    tap_count = conv_weight.shape[0]
    channel_count = conv_weight.shape[1]
    head_count = rate_log.shape[0]
    inner_width = gate_input.shape[2]
    head_width = inner_width // head_count
    state_width = (channel_count - inner_width) // 2
    model_width = residual.shape[2]
    edge_rows = frames_in[row_count - (tap_count - 1) :]
    before = from_behind(edge_rows, "seq", 1)
    padded = jnp.concatenate([before, frames_in], axis=0).astype(jnp.float32)
    summed = conv_weight[0][None, :] * padded[0:row_count]
    for offset in range(1, tap_count):
        summed = summed + conv_weight[offset][None, :] * padded[offset : offset + row_count]
    signal = jax.nn.silu(summed).astype(jnp.bfloat16)
    x_part = signal[:, :inner_width]
    b_part = signal[:, inner_width : inner_width + state_width]
    c_part = signal[:, inner_width + state_width :]
    step_size = jax.nn.softplus(step_raw[0])
    log_decay = -step_size * jnp.exp(rate_log)[None, :]
    cumulative = jnp.cumsum(log_decay, axis=0)
    x_values = x_part.astype(jnp.float32).reshape(row_count, head_count, head_width)
    b_values = b_part.astype(jnp.float32)
    c_values = c_part.astype(jnp.float32)
    scores = jnp.dot(c_part, b_part.T, preferred_element_type=jnp.float32)
    positions = jnp.arange(row_count)
    causal = positions[:, None] >= positions[None, :]
    by_head = cumulative.T
    gap_log = by_head[:, :, None] - by_head[:, None, :]
    decay_mask = jnp.where(causal[None], jnp.exp(jnp.where(causal[None], gap_log, 0.0)), 0.0)
    mixing = (scores[None] * decay_mask * step_size.T[:, None, :]).astype(half)
    x_heads = x_part.reshape(row_count, head_count, head_width)
    tail_weight = jnp.exp(cumulative[-1][None, :] - cumulative) * step_size
    local_state = jnp.einsum(
        "shp,sn->hpn",
        (x_values * tail_weight[:, :, None]).astype(half),
        b_part,
        preferred_element_type=jnp.float32,
    ).astype(half)
    totals = lax.all_gather(cumulative[-1], "seq", axis=0)
    passing = jnp.zeros_like(totals[0])
    entering = jnp.zeros(local_state.shape, jnp.float32)
    for shift in range(1, ring):
        arrived_state = from_behind(local_state, "seq", shift).astype(jnp.float32)
        entering = entering + jnp.exp(passing)[:, None, None] * arrived_state
        passing = passing + totals[jnp.maximum(own - shift, 0)]
    within = jnp.einsum("hts,shp->thp", mixing, x_heads, preferred_element_type=jnp.float32)
    carried = (
        jnp.einsum("tn,hpn->thp", c_part, entering.astype(half), preferred_element_type=jnp.float32)
        * jnp.exp(cumulative)[:, :, None]
    )
    ssd_out = (within + carried + skip_gain[None, :, None] * x_values).reshape(
        row_count, inner_width
    )
    gated_out = ssd_out * jax.nn.silu(gate_input[0].astype(jnp.float32))
    mean_square = jnp.mean(gated_out * gated_out, axis=1, keepdims=True)
    normed = (gated_out * lax.rsqrt(mean_square + EPSILON) * norm_gain[None, :]).astype(
        jnp.bfloat16
    )
    all_rows = lax.all_gather(normed, "seq", axis=0, tiled=True)
    column_share = jnp.dot(all_rows, weight_share, preferred_element_type=jnp.float32).astype(half)
    projected = lax.all_to_all(column_share, "seq", split_axis=0, concat_axis=1, tiled=True).astype(
        jnp.float32
    )
    mixed_out = (residual[0].astype(jnp.float32) + projected).astype(jnp.bfloat16)
    mixed_float = mixed_out.astype(jnp.float32)
    mixed_square = jnp.mean(mixed_float * mixed_float, axis=1, keepdims=True)
    moe_in = (mixed_float * lax.rsqrt(mixed_square + EPSILON) * moe_gain[None, :]).astype(
        jnp.bfloat16
    )
    experts = lax.axis_size("grp")
    capacity = 4 * row_count // experts
    flat_picks = routes[0].reshape(-1)
    member = (flat_picks[:, None] == jnp.arange(experts)[None, :]).astype(jnp.int32)
    position = jnp.cumsum(member, axis=0) - member
    slot_index = jnp.sum(position * member, axis=1)
    target = (flat_picks * capacity + slot_index).reshape(row_count, 2)
    selector = jnp.any(
        target[None, :, :] == jnp.arange(experts * capacity)[:, None, None], axis=2
    ).astype(jnp.bfloat16)
    outgoing = (
        jnp.dot(selector, moe_in, preferred_element_type=jnp.float32)
        .astype(jnp.bfloat16)
        .reshape(experts, capacity, model_width)
    )
    gate_matrix = w_gate[0]
    up_matrix = w_up[0]
    down_matrix = w_down[0]
    arrived = lax.all_to_all(outgoing, "grp", split_axis=0, concat_axis=0, tiled=True)
    flattened_rows = arrived.reshape(-1, model_width)
    gate_part = jnp.dot(flattened_rows, gate_matrix, preferred_element_type=jnp.float32)
    up_part = jnp.dot(flattened_rows, up_matrix, preferred_element_type=jnp.float32)
    expert_hidden = (jax.nn.silu(gate_part) * up_part).astype(jnp.bfloat16)
    result = (
        jnp.dot(expert_hidden, down_matrix, preferred_element_type=jnp.float32)
        .astype(jnp.bfloat16)
        .reshape(arrived.shape)
    )
    returned = lax.all_to_all(result, "grp", split_axis=0, concat_axis=0, tiled=True)
    back_rows = returned.reshape(experts * capacity, model_width)
    slots = jnp.arange(experts * capacity)[None, :]
    first_pick = (target[:, 0:1] == slots).astype(half)
    second_pick = (target[:, 1:2] == slots).astype(half)
    first_out = jnp.dot(first_pick, back_rows, preferred_element_type=jnp.float32)
    second = jnp.dot(second_pick, back_rows, preferred_element_type=jnp.float32)
    pair_weights = route_weights[0]
    layer_out = mixed_float + pair_weights[:, 0:1] * first_out + pair_weights[:, 1:2] * second
    return layer_out.astype(jnp.bfloat16)[None]


def solution(mesh):
    in_specs = (
        P("grp", "seq", None),
        P(),
        P("grp", "seq", None),
        P(),
        P(),
        P("grp", "seq", None),
        P(),
        P("grp", None),
        P("grp", "seq", None),
        P(),
        P("grp", None, None),
        P("grp", None, None),
        P("grp", None, None),
        P("grp", "seq", None),
        P("grp", "seq", None),
    )
    out_specs = P("grp", "seq", None)
    return jax.shard_map(
        on_device, mesh=mesh, in_specs=in_specs, out_specs=out_specs, check_vma=False
    )
```

```python
import functools

import jax
import jax.numpy as jnp
from jax import lax
from jax.experimental import pallas as pl
from jax.experimental.pallas import tpu as pltpu
from jax.sharding import PartitionSpec as P

EPSILON = 1e-05


def from_behind(value, axis, steps):
    count = lax.axis_size(axis)
    first, last = (max(0, -steps), min(count, count - steps))
    return lax.ppermute(value, axis, [(source, source + steps) for source in range(first, last)])


def exchange_kernel(
    ring,
    experts,
    normed_ref,
    weight_hbm,
    residual_ref,
    gain_ref,
    gate_hbm,
    up_hbm,
    down_hbm,
    send_pick_ref,
    first_pick_ref,
    second_pick_ref,
    pair_ref,
    out_ref,
    weight_ref,
    gate_ref,
    up_ref,
    down_ref,
    rows_in,
    share_out,
    share_in,
    mixed_ref,
    moe_ref,
    outgoing,
    arrived,
    result,
    returned,
    local_sem,
    rows_send,
    rows_recv,
    share_send,
    share_recv,
    out_send,
    out_recv,
    back_send,
    back_recv,
):
    me = lax.axis_index("seq")
    mine = lax.axis_index("grp")
    width = moe_ref.shape[1]
    stretch = 512 if width % 512 == 0 else 128
    share = weight_ref.shape[1]
    capacity = outgoing.shape[1]
    half = jnp.bfloat16
    full = jnp.float32

    locals_ = [
        pltpu.make_async_copy(source, target, local_sem.at[index])
        for index, (source, target) in enumerate(
            ((weight_hbm, weight_ref), (gate_hbm, gate_ref), (up_hbm, up_ref), (down_hbm, down_ref))
        )
    ]
    for copy in locals_:
        copy.start()

    barrier = pltpu.get_barrier_semaphore()

    def greet(axis, own, count):
        def step(shift, carry):
            pl.semaphore_signal(
                barrier,
                inc=1,
                device_id={axis: lax.rem(own + shift, count)},
                device_id_type=pl.DeviceIdType.MESH,
            )
            return carry

        lax.fori_loop(1, count, step, 0)

    greet("seq", me, ring)
    greet("grp", mine, experts)
    pl.semaphore_wait(barrier, ring - 1 + experts - 1)

    def rows_copy(shift):
        return pltpu.make_async_remote_copy(
            src_ref=normed_ref,
            dst_ref=rows_in.at[shift],
            send_sem=rows_send.at[shift],
            recv_sem=rows_recv.at[shift],
            device_id={"seq": lax.rem(me + shift, ring)},
            device_id_type=pl.DeviceIdType.MESH,
        )

    def share_copy(shift):
        return pltpu.make_async_remote_copy(
            src_ref=share_out.at[shift],
            dst_ref=share_in.at[shift],
            send_sem=share_send.at[shift],
            recv_sem=share_recv.at[shift],
            device_id={"seq": lax.rem(me + ring - shift, ring)},
            device_id_type=pl.DeviceIdType.MESH,
        )

    def out_copy(shift):
        return pltpu.make_async_remote_copy(
            src_ref=outgoing.at[shift],
            dst_ref=arrived.at[shift],
            send_sem=out_send.at[shift],
            recv_sem=out_recv.at[shift],
            device_id={"grp": lax.rem(mine + shift, experts)},
            device_id_type=pl.DeviceIdType.MESH,
        )

    def back_copy(shift):
        return pltpu.make_async_remote_copy(
            src_ref=result.at[shift],
            dst_ref=returned.at[shift],
            send_sem=back_send.at[shift],
            recv_sem=back_recv.at[shift],
            device_id={"grp": lax.rem(mine + experts - shift, experts)},
            device_id_type=pl.DeviceIdType.MESH,
        )

    def send_rows(shift, carry):
        rows_copy(shift).start()
        return carry

    lax.fori_loop(1, ring, send_rows, 0)
    rows_in[0] = normed_ref[...]
    locals_[0].wait()

    def project(shift, carry):
        @pl.when(shift > 0)
        def _():
            rows_copy(shift).wait_recv()

        share_out[shift] = jnp.dot(
            rows_in[shift], weight_ref[...], preferred_element_type=full
        ).astype(half)

        @pl.when(shift > 0)
        def _():
            share_copy(shift).start()

        return carry

    lax.fori_loop(0, ring, project, 0)
    share_in[0] = share_out[0]

    def mix(shift, squares):
        @pl.when(shift > 0)
        def _():
            share_copy(shift).wait_recv()

        column = pl.multiple_of(lax.rem(me + shift, ring) * share, share)
        values = (
            residual_ref[:, pl.ds(column, share)].astype(full) + share_in[shift].astype(full)
        ).astype(half)
        mixed_ref[:, pl.ds(column, share)] = values
        wide = values.astype(full)
        return squares + jnp.sum(wide * wide, axis=1, keepdims=True)

    squares = lax.fori_loop(0, ring, mix, jnp.zeros((mixed_ref.shape[0], 1), full))
    scale = lax.rsqrt(squares * (1.0 / width) + EPSILON)
    moe_ref[...] = (mixed_ref[:, :width].astype(full) * scale * gain_ref[...]).astype(half)

    def dispatch(shift, carry):
        outgoing[shift] = jnp.dot(
            send_pick_ref[shift], moe_ref[...], preferred_element_type=full
        ).astype(half)

        @pl.when(shift > 0)
        def _():
            out_copy(shift).start()

        return carry

    lax.fori_loop(1, experts, dispatch, 0)
    arrived[0] = jnp.dot(send_pick_ref[0], moe_ref[...], preferred_element_type=full).astype(half)
    for copy in locals_[1:]:
        copy.wait()

    def run_expert(pair, carry):
        low = pair * 2

        @pl.when(low > 0)
        def _():
            out_copy(low).wait_recv()

        out_copy(low + 1).wait_recv()
        rows = arrived[pl.ds(low, 2)].reshape(2 * capacity, width)
        gate_part = jnp.dot(rows, gate_ref[...], preferred_element_type=full)
        up_part = jnp.dot(rows, up_ref[...], preferred_element_type=full)
        hidden = (gate_part * jax.nn.sigmoid(gate_part) * up_part).astype(half)
        made = jnp.dot(hidden, down_ref[...], preferred_element_type=full).astype(half)
        result[pl.ds(low, 2)] = made.reshape(2, capacity, width)

        @pl.when(low > 0)
        def _():
            back_copy(low).start()

        back_copy(low + 1).start()
        return carry

    lax.fori_loop(0, experts // 2, run_expert, 0)
    returned[0] = result[0]

    def take_back(shift, carry):
        back_copy(shift).wait_recv()
        return carry

    lax.fori_loop(1, experts, take_back, 0)
    first_weight = pair_ref[:, 0:1]
    second_weight = pair_ref[:, 1:2]

    def combine(tile, carry):
        column = pl.multiple_of(tile * stretch, stretch)
        rows = returned[:, :, pl.ds(column, stretch)].reshape(experts * capacity, stretch)
        first = jnp.dot(first_pick_ref[...], rows, preferred_element_type=full)
        second = jnp.dot(second_pick_ref[...], rows, preferred_element_type=full)
        out_ref[:, pl.ds(column, stretch)] = (
            mixed_ref[:, pl.ds(column, stretch)].astype(full)
            + first_weight * first
            + second_weight * second
        ).astype(half)
        return carry

    lax.fori_loop(0, width // stretch, combine, 0)

    def drain_seq(shift, carry):
        rows_copy(shift).wait_send()
        share_copy(shift).wait_send()
        return carry

    def drain_grp(shift, carry):
        out_copy(shift).wait_send()
        back_copy(shift).wait_send()
        return carry

    lax.fori_loop(1, ring, drain_seq, 0)
    lax.fori_loop(1, experts, drain_grp, 0)


def on_device(
    conv_input,
    conv_weight,
    step_raw,
    rate_log,
    skip_gain,
    gate_input,
    norm_gain,
    out_weight,
    residual,
    moe_gain,
    w_gate,
    w_up,
    w_down,
    routes,
    route_weights,
):
    half = jnp.bfloat16
    ring = lax.axis_size("seq")
    own = lax.axis_index("seq")
    share = -(-out_weight.shape[1] // (ring * 128)) * 128
    extra = ring * share - out_weight.shape[1]
    weight_part = lax.dynamic_slice_in_dim(
        jnp.pad(out_weight, ((0, 0), (0, extra))), own * share, share, axis=1
    )
    weight_part, conv_input = lax.optimization_barrier((weight_part, conv_input))
    weight_share = lax.all_gather(weight_part, "grp", axis=0, tiled=True)
    frames_in = conv_input[0]
    row_count = frames_in.shape[0]
    tap_count = conv_weight.shape[0]
    channel_count = conv_weight.shape[1]
    head_count = rate_log.shape[0]
    inner_width = gate_input.shape[2]
    head_width = inner_width // head_count
    state_width = (channel_count - inner_width) // 2
    model_width = residual.shape[2]
    edge_rows = frames_in[row_count - (tap_count - 1) :]
    before = from_behind(edge_rows, "seq", 1)
    padded = jnp.concatenate([before, frames_in], axis=0).astype(jnp.float32)
    summed = conv_weight[0][None, :] * padded[0:row_count]
    for offset in range(1, tap_count):
        summed = summed + conv_weight[offset][None, :] * padded[offset : offset + row_count]
    signal = jax.nn.silu(summed).astype(jnp.bfloat16)
    x_part = signal[:, :inner_width]
    b_part = signal[:, inner_width : inner_width + state_width]
    c_part = signal[:, inner_width + state_width :]
    step_size = jax.nn.softplus(step_raw[0])
    log_decay = -step_size * jnp.exp(rate_log)[None, :]
    cumulative = jnp.cumsum(log_decay, axis=0)
    x_values = x_part.astype(jnp.float32).reshape(row_count, head_count, head_width)
    b_values = b_part.astype(jnp.float32)
    c_values = c_part.astype(jnp.float32)
    scores = jnp.dot(c_part, b_part.T, preferred_element_type=jnp.float32)
    positions = jnp.arange(row_count)
    causal = positions[:, None] >= positions[None, :]
    by_head = cumulative.T
    gap_log = by_head[:, :, None] - by_head[:, None, :]
    decay_mask = jnp.where(causal[None], jnp.exp(jnp.where(causal[None], gap_log, 0.0)), 0.0)
    mixing = (scores[None] * decay_mask * step_size.T[:, None, :]).astype(half)
    x_heads = x_part.reshape(row_count, head_count, head_width)
    tail_weight = jnp.exp(cumulative[-1][None, :] - cumulative) * step_size
    local_state = jnp.einsum(
        "shp,sn->hpn",
        (x_values * tail_weight[:, :, None]).astype(half),
        b_part,
        preferred_element_type=jnp.float32,
    ).astype(half)
    totals = lax.all_gather(cumulative[-1], "seq", axis=0)
    passing = jnp.zeros_like(totals[0])
    entering = jnp.zeros(local_state.shape, jnp.float32)
    for shift in range(1, ring):
        arrived_state = from_behind(local_state, "seq", shift).astype(jnp.float32)
        entering = entering + jnp.exp(passing)[:, None, None] * arrived_state
        passing = passing + totals[jnp.maximum(own - shift, 0)]
    within = jnp.einsum("hts,shp->thp", mixing, x_heads, preferred_element_type=jnp.float32)
    carried = (
        jnp.einsum("tn,hpn->thp", c_part, entering.astype(half), preferred_element_type=jnp.float32)
        * jnp.exp(cumulative)[:, :, None]
    )
    ssd_out = (within + carried + skip_gain[None, :, None] * x_values).reshape(
        row_count, inner_width
    )
    gated_out = ssd_out * jax.nn.silu(gate_input[0].astype(jnp.float32))
    mean_square = jnp.mean(gated_out * gated_out, axis=1, keepdims=True)
    normed = (gated_out * lax.rsqrt(mean_square + EPSILON) * norm_gain[None, :]).astype(
        jnp.bfloat16
    )
    experts = lax.axis_size("grp")
    capacity = 4 * row_count // experts
    flat_picks = (routes[0].reshape(-1) - lax.axis_index("grp") + experts) % experts
    member = (flat_picks[:, None] == jnp.arange(experts)[None, :]).astype(jnp.int32)
    position = jnp.cumsum(member, axis=0) - member
    slot_index = jnp.sum(position * member, axis=1)
    target = (flat_picks * capacity + slot_index).reshape(row_count, 2)
    slots = jnp.arange(experts * capacity)
    send_pick = (
        jnp.any(target[None, :, :] == slots[:, None, None], axis=2)
        .astype(half)
        .reshape(experts, capacity, row_count)
    )
    first_pick = (target[:, 0:1] == slots[None, :]).astype(half)
    second_pick = (target[:, 1:2] == slots[None, :]).astype(half)
    hidden_width = w_gate.shape[2]
    vmem = pl.BlockSpec(memory_space=pltpu.VMEM)
    anywhere = pl.BlockSpec(memory_space=pl.ANY)
    slab = pltpu.VMEM((experts, capacity, model_width), half)
    piece = pltpu.VMEM((ring, row_count, share), half)
    whole_rows = pltpu.VMEM((row_count, model_width), half)
    layer_out = pl.pallas_call(
        functools.partial(exchange_kernel, ring, experts),
        out_shape=jax.ShapeDtypeStruct((row_count, model_width), half),
        in_specs=[vmem, anywhere, vmem, vmem, anywhere, anywhere, anywhere, vmem, vmem, vmem, vmem],
        out_specs=vmem,
        scratch_shapes=[
            pltpu.VMEM((inner_width, share), half),
            pltpu.VMEM((model_width, hidden_width), half),
            pltpu.VMEM((model_width, hidden_width), half),
            pltpu.VMEM((hidden_width, model_width), half),
            pltpu.VMEM((ring, row_count, inner_width), half),
            piece,
            piece,
            pltpu.VMEM((row_count, ring * share), half),
            whole_rows,
            slab,
            slab,
            slab,
            slab,
            pltpu.SemaphoreType.DMA((4,)),
        ]
        + [pltpu.SemaphoreType.DMA((ring,))] * 4
        + [pltpu.SemaphoreType.DMA((experts,))] * 4,
        compiler_params=pltpu.CompilerParams(
            collective_id=0, has_side_effects=True, vmem_limit_bytes=48 * 1024 * 1024
        ),
        cost_estimate=pl.CostEstimate(
            flops=6 * 1024 * 1024 * 1024, bytes_accessed=64 * 1024 * 1024, transcendentals=0
        ),
    )(
        normed,
        weight_share,
        jnp.pad(residual[0], ((0, 0), (0, extra))),
        moe_gain[None, :],
        w_gate[0],
        w_up[0],
        w_down[0],
        send_pick,
        first_pick,
        second_pick,
        route_weights[0],
    )
    return layer_out[None]


def solution(mesh):
    in_specs = (
        P("grp", "seq", None),
        P(),
        P("grp", "seq", None),
        P(),
        P(),
        P("grp", "seq", None),
        P(),
        P("grp", None),
        P("grp", "seq", None),
        P(),
        P("grp", None, None),
        P("grp", None, None),
        P("grp", None, None),
        P("grp", "seq", None),
        P("grp", "seq", None),
    )
    out_specs = P("grp", "seq", None)
    return jax.shard_map(
        on_device, mesh=mesh, in_specs=in_specs, out_specs=out_specs, check_vma=False
    )
```

```python
import functools

import jax
import jax.numpy as jnp
from jax import lax
from jax.experimental import pallas as pl
from jax.experimental.pallas import tpu as pltpu
from jax.sharding import PartitionSpec as P

EPSILON = 1e-05


def from_behind(value, axis, steps):
    count = lax.axis_size(axis)
    first, last = (max(0, -steps), min(count, count - steps))
    return lax.ppermute(value, axis, [(source, source + steps) for source in range(first, last)])


def mixer_kernel(
    chips,
    state_ref,
    reach_ref,
    c_ref,
    base_ref,
    fade_ref,
    gate_ref,
    gain_ref,
    rows_ref,
    gated,
    states,
    near_state_send,
    far_state_send,
    state_recv,
    near_rows_send,
    far_rows_send,
    rows_recv,
):
    me = lax.axis_index("seq")
    chip, core = me // 2, me % 2
    twin = chip * 2 + 1 - core
    half = jnp.bfloat16
    full = jnp.float32

    def far(step):
        return lax.rem(chip + step, chips) * 2 + core

    barrier = pltpu.get_barrier_semaphore()

    def greet(device):
        pl.semaphore_signal(
            barrier, inc=1, device_id={"seq": device}, device_id_type=pl.DeviceIdType.MESH
        )

    greet(twin)
    for step in range(1, chips):
        greet(far(step))
    pl.semaphore_wait(barrier, chips)

    def copy(slots, near_send, far_send, recv, step, near):
        return pltpu.make_async_remote_copy(
            src_ref=slots.at[2 * step] if near else slots.at[0],
            dst_ref=slots.at[2 * step + 1] if near else slots.at[2 * step],
            send_sem=near_send.at[step] if near else far_send.at[step],
            recv_sem=recv.at[2 * step + 1] if near else recv.at[2 * step],
            device_id={"seq": twin if near else far(step)},
            device_id_type=pl.DeviceIdType.MESH,
        )

    def exchange(*parts):
        for step in range(1, chips):
            copy(*parts, step, False).start()
        copy(*parts, 0, True).start()
        for step in range(1, chips):
            copy(*parts, step, False).wait_recv()
            copy(*parts, step, True).start()
        for step in range(chips):
            copy(*parts, step, True).wait_recv()

    def drain(*parts):
        for step in range(1, chips):
            copy(*parts, step, False).wait_send()
        for step in range(chips):
            copy(*parts, step, True).wait_send()

    state_parts = (states, near_state_send, far_state_send, state_recv)
    rows_parts = (rows_ref, near_rows_send, far_rows_send, rows_recv)
    states[0] = state_ref[...]
    exchange(*state_parts)
    width = gate_ref.shape[1]
    stretch = 512 if width % 512 == 0 else 128
    squares = jnp.zeros((gate_ref.shape[0], 1), full)
    for start in range(0, width, stretch):
        columns = slice(start, start + stretch)
        entering = jnp.zeros((states.shape[1], stretch), full)
        for slot in range(1, 2 * chips):
            entering = entering + reach_ref[slot : slot + 1, columns] * states[
                slot, :, columns
            ].astype(full)
        carried = jnp.dot(c_ref[...], entering.astype(half), preferred_element_type=full)
        gate = gate_ref[:, columns].astype(full)
        value = (base_ref[:, columns] + carried * fade_ref[:, columns]) * (
            gate * jax.nn.sigmoid(gate)
        )
        gated[:, columns] = value
        squares = squares + jnp.sum(value * value, axis=1, keepdims=True)
    scale = lax.rsqrt(squares * (1.0 / width) + EPSILON)
    for start in range(0, width, stretch):
        columns = slice(start, start + stretch)
        rows_ref[0, :, columns] = (gated[:, columns] * scale * gain_ref[:, columns]).astype(half)
    exchange(*rows_parts)
    drain(*state_parts)
    drain(*rows_parts)


def exchange_kernel(
    ring,
    experts,
    rows_ref,
    weight_hbm,
    residual_ref,
    gain_ref,
    gate_hbm,
    up_hbm,
    down_hbm,
    send_pick_ref,
    first_pick_ref,
    second_pick_ref,
    pair_ref,
    out_ref,
    weight_ref,
    gate_ref,
    up_ref,
    down_ref,
    share_out,
    share_in,
    mixed_ref,
    moe_ref,
    outgoing,
    arrived,
    result,
    returned,
    local_sem,
    share_send,
    share_recv,
    out_send,
    out_recv,
    back_send,
    back_recv,
):
    me = lax.axis_index("seq")
    mine = lax.axis_index("grp")
    width = moe_ref.shape[1]
    stretch = 512 if width % 512 == 0 else 128
    share = weight_ref.shape[1]
    capacity = outgoing.shape[1]
    half = jnp.bfloat16
    full = jnp.float32

    locals_ = [
        pltpu.make_async_copy(source, target, local_sem.at[index])
        for index, (source, target) in enumerate(
            ((weight_hbm, weight_ref), (gate_hbm, gate_ref), (up_hbm, up_ref), (down_hbm, down_ref))
        )
    ]
    for copy in locals_:
        copy.start()

    barrier = pltpu.get_barrier_semaphore()

    def greet(axis, own, count):
        def step(shift, carry):
            pl.semaphore_signal(
                barrier,
                inc=1,
                device_id={axis: lax.rem(own + shift, count)},
                device_id_type=pl.DeviceIdType.MESH,
            )
            return carry

        lax.fori_loop(1, count, step, 0)

    greet("seq", me, ring)
    greet("grp", mine, experts)
    pl.semaphore_wait(barrier, ring - 1 + experts - 1)

    def source(slot):
        chips = ring // 2
        chip = lax.rem(me // 2 + chips - slot // 2, chips)
        return chip * 2 + lax.rem(me + slot, 2)

    def share_copy(slot):
        return pltpu.make_async_remote_copy(
            src_ref=share_out.at[slot],
            dst_ref=share_in.at[me],
            send_sem=share_send.at[slot],
            recv_sem=share_recv.at[me],
            device_id={"seq": source(slot)},
            device_id_type=pl.DeviceIdType.MESH,
        )

    def share_arrival(column):
        return pltpu.make_async_remote_copy(
            src_ref=share_out.at[0],
            dst_ref=share_in.at[column],
            send_sem=share_send.at[0],
            recv_sem=share_recv.at[column],
            device_id={"seq": source(1)},
            device_id_type=pl.DeviceIdType.MESH,
        )

    def out_copy(shift):
        return pltpu.make_async_remote_copy(
            src_ref=outgoing.at[shift],
            dst_ref=arrived.at[shift],
            send_sem=out_send.at[shift],
            recv_sem=out_recv.at[shift],
            device_id={"grp": lax.rem(mine + shift, experts)},
            device_id_type=pl.DeviceIdType.MESH,
        )

    def back_copy(shift):
        return pltpu.make_async_remote_copy(
            src_ref=result.at[shift],
            dst_ref=returned.at[shift],
            send_sem=back_send.at[shift],
            recv_sem=back_recv.at[shift],
            device_id={"grp": lax.rem(mine + experts - shift, experts)},
            device_id_type=pl.DeviceIdType.MESH,
        )

    locals_[0].wait()

    def project(index, carry):
        slot = ring - 1 - index
        share_out[slot] = jnp.dot(
            rows_ref[slot], weight_ref[...], preferred_element_type=full
        ).astype(half)

        @pl.when(slot > 0)
        def _():
            share_copy(slot).start()

        return carry

    lax.fori_loop(0, ring, project, 0)
    share_in[me] = share_out[0]

    def mix(index, squares):
        @pl.when(index != me)
        def _():
            share_arrival(index).wait_recv()

        column = pl.multiple_of(index * share, share)
        values = (
            residual_ref[:, pl.ds(column, share)].astype(full) + share_in[index].astype(full)
        ).astype(half)
        mixed_ref[:, pl.ds(column, share)] = values
        wide = values.astype(full)
        return squares + jnp.sum(wide * wide, axis=1, keepdims=True)

    squares = lax.fori_loop(0, ring, mix, jnp.zeros((mixed_ref.shape[0], 1), full))
    scale = lax.rsqrt(squares * (1.0 / width) + EPSILON)
    moe_ref[...] = (mixed_ref[:, :width].astype(full) * scale * gain_ref[...]).astype(half)

    def dispatch(shift, carry):
        outgoing[shift] = jnp.dot(
            send_pick_ref[shift], moe_ref[...], preferred_element_type=full
        ).astype(half)

        @pl.when(shift > 0)
        def _():
            out_copy(shift).start()

        return carry

    lax.fori_loop(1, experts, dispatch, 0)
    arrived[0] = jnp.dot(send_pick_ref[0], moe_ref[...], preferred_element_type=full).astype(half)
    for copy in locals_[1:]:
        copy.wait()

    def run_expert(pair, carry):
        low = pair * 2

        @pl.when(low > 0)
        def _():
            out_copy(low).wait_recv()

        out_copy(low + 1).wait_recv()
        rows = arrived[pl.ds(low, 2)].reshape(2 * capacity, width)
        gate_part = jnp.dot(rows, gate_ref[...], preferred_element_type=full)
        up_part = jnp.dot(rows, up_ref[...], preferred_element_type=full)
        hidden = (gate_part * jax.nn.sigmoid(gate_part) * up_part).astype(half)
        made = jnp.dot(hidden, down_ref[...], preferred_element_type=full).astype(half)
        result[pl.ds(low, 2)] = made.reshape(2, capacity, width)

        @pl.when(low > 0)
        def _():
            back_copy(low).start()

        back_copy(low + 1).start()
        return carry

    lax.fori_loop(0, experts // 2, run_expert, 0)
    returned[0] = result[0]

    def take_back(shift, carry):
        back_copy(shift).wait_recv()
        return carry

    lax.fori_loop(1, experts, take_back, 0)
    first_weight = pair_ref[:, 0:1]
    second_weight = pair_ref[:, 1:2]

    def combine(tile, carry):
        column = pl.multiple_of(tile * stretch, stretch)
        rows = returned[:, :, pl.ds(column, stretch)].reshape(experts * capacity, stretch)
        first = jnp.dot(first_pick_ref[...], rows, preferred_element_type=full)
        second = jnp.dot(second_pick_ref[...], rows, preferred_element_type=full)
        out_ref[:, pl.ds(column, stretch)] = (
            mixed_ref[:, pl.ds(column, stretch)].astype(full)
            + first_weight * first
            + second_weight * second
        ).astype(half)
        return carry

    lax.fori_loop(0, width // stretch, combine, 0)

    def drain_seq(shift, carry):
        share_copy(shift).wait_send()
        return carry

    def drain_grp(shift, carry):
        out_copy(shift).wait_send()
        back_copy(shift).wait_send()
        return carry

    lax.fori_loop(1, ring, drain_seq, 0)
    lax.fori_loop(1, experts, drain_grp, 0)


def on_device(
    conv_input,
    conv_weight,
    step_raw,
    rate_log,
    skip_gain,
    gate_input,
    norm_gain,
    out_weight,
    residual,
    moe_gain,
    w_gate,
    w_up,
    w_down,
    routes,
    route_weights,
):
    half = jnp.bfloat16
    ring = lax.axis_size("seq")
    own = lax.axis_index("seq")
    share = -(-out_weight.shape[1] // (ring * 128)) * 128
    extra = ring * share - out_weight.shape[1]
    weight_part = lax.dynamic_slice_in_dim(
        jnp.pad(out_weight, ((0, 0), (0, extra))), own * share, share, axis=1
    )
    weight_part, conv_input = lax.optimization_barrier((weight_part, conv_input))
    weight_share = lax.all_gather(weight_part, "grp", axis=0, tiled=True)
    frames_in = conv_input[0]
    row_count = frames_in.shape[0]
    tap_count = conv_weight.shape[0]
    channel_count = conv_weight.shape[1]
    head_count = rate_log.shape[0]
    inner_width = gate_input.shape[2]
    head_width = inner_width // head_count
    state_width = (channel_count - inner_width) // 2
    model_width = residual.shape[2]
    edge_rows = frames_in[row_count - (tap_count - 1) :]
    before = from_behind(edge_rows, "seq", 1)
    padded = jnp.concatenate([before, frames_in], axis=0).astype(jnp.float32)
    summed = conv_weight[0][None, :] * padded[0:row_count]
    for offset in range(1, tap_count):
        summed = summed + conv_weight[offset][None, :] * padded[offset : offset + row_count]
    signal = jax.nn.silu(summed).astype(jnp.bfloat16)
    x_part = signal[:, :inner_width]
    b_part = signal[:, inner_width : inner_width + state_width]
    c_part = signal[:, inner_width + state_width :]
    step_size = jax.nn.softplus(step_raw[0])
    log_decay = -step_size * jnp.exp(rate_log)[None, :]
    cumulative = jnp.cumsum(log_decay, axis=0)
    x_float = x_part.astype(jnp.float32)
    scores = jnp.dot(c_part, b_part.T, preferred_element_type=jnp.float32)
    positions = jnp.arange(row_count)
    causal = positions[:, None] >= positions[None, :]
    by_head = cumulative.T
    gap_log = by_head[:, :, None] - by_head[:, None, :]
    decay_mask = jnp.where(causal[None], jnp.exp(jnp.where(causal[None], gap_log, 0.0)), 0.0)
    mixing = (scores[None] * decay_mask * step_size.T[:, None, :]).astype(half)
    x_heads = x_part.reshape(row_count, head_count, head_width)
    tail_weight = jnp.exp(cumulative[-1][None, :] - cumulative) * step_size
    local_state = lax.dot_general(
        b_part,
        (x_float * jnp.repeat(tail_weight, head_width, axis=1)).astype(half),
        (((0,), (0,)), ((), ())),
        preferred_element_type=jnp.float32,
    ).astype(half)
    totals = lax.all_gather(cumulative[-1], "seq", axis=0)
    slot_ids = jnp.arange(ring)
    origin = (own // 2 - slot_ids // 2 + ring // 2) % (ring // 2) * 2 + (own + slot_ids) % 2
    between = (slot_ids[None, :] > origin[:, None]) & (slot_ids[None, :] < own)
    passed = jnp.sum(jnp.where(between[:, :, None], totals[None], 0.0), axis=1)
    reach = jnp.where((origin < own)[:, None], jnp.exp(passed), 0.0)
    within = jnp.einsum("hts,shp->thp", mixing, x_heads, preferred_element_type=jnp.float32)
    base = within.reshape(row_count, inner_width) + jnp.repeat(skip_gain, head_width)[None, :] * x_float
    vmem = pl.BlockSpec(memory_space=pltpu.VMEM)
    all_rows = pl.pallas_call(
        functools.partial(mixer_kernel, ring // 2),
        out_shape=jax.ShapeDtypeStruct((ring, row_count, inner_width), half),
        in_specs=[vmem] * 7,
        out_specs=vmem,
        scratch_shapes=[
            pltpu.VMEM((row_count, inner_width), jnp.float32),
            pltpu.VMEM((ring, state_width, inner_width), half),
        ]
        + [
            pltpu.SemaphoreType.DMA((ring // 2,)),
            pltpu.SemaphoreType.DMA((ring // 2,)),
            pltpu.SemaphoreType.DMA((ring,)),
        ]
        * 2,
        compiler_params=pltpu.CompilerParams(
            collective_id=1, has_side_effects=True, vmem_limit_bytes=32 * 1024 * 1024
        ),
        cost_estimate=pl.CostEstimate(
            flops=1024 * 1024 * 1024, bytes_accessed=64 * 1024 * 1024, transcendentals=0
        ),
    )(
        local_state,
        jnp.repeat(reach, head_width, axis=1),
        c_part,
        base,
        jnp.repeat(jnp.exp(cumulative), head_width, axis=1),
        gate_input[0],
        norm_gain[None, :],
    )
    experts = lax.axis_size("grp")
    capacity = 4 * row_count // experts
    flat_picks = (routes[0].reshape(-1) - lax.axis_index("grp") + experts) % experts
    member = (flat_picks[:, None] == jnp.arange(experts)[None, :]).astype(jnp.int32)
    position = jnp.cumsum(member, axis=0) - member
    slot_index = jnp.sum(position * member, axis=1)
    target = (flat_picks * capacity + slot_index).reshape(row_count, 2)
    slots = jnp.arange(experts * capacity)
    send_pick = (
        jnp.any(target[None, :, :] == slots[:, None, None], axis=2)
        .astype(half)
        .reshape(experts, capacity, row_count)
    )
    first_pick = (target[:, 0:1] == slots[None, :]).astype(half)
    second_pick = (target[:, 1:2] == slots[None, :]).astype(half)
    hidden_width = w_gate.shape[2]
    anywhere = pl.BlockSpec(memory_space=pl.ANY)
    slab = pltpu.VMEM((experts, capacity, model_width), half)
    piece = pltpu.VMEM((ring, row_count, share), half)
    whole_rows = pltpu.VMEM((row_count, model_width), half)
    layer_out = pl.pallas_call(
        functools.partial(exchange_kernel, ring, experts),
        out_shape=jax.ShapeDtypeStruct((row_count, model_width), half),
        in_specs=[vmem, anywhere, vmem, vmem, anywhere, anywhere, anywhere, vmem, vmem, vmem, vmem],
        out_specs=vmem,
        scratch_shapes=[
            pltpu.VMEM((inner_width, share), half),
            pltpu.VMEM((model_width, hidden_width), half),
            pltpu.VMEM((model_width, hidden_width), half),
            pltpu.VMEM((hidden_width, model_width), half),
            piece,
            piece,
            pltpu.VMEM((row_count, ring * share), half),
            whole_rows,
            slab,
            slab,
            slab,
            slab,
            pltpu.SemaphoreType.DMA((4,)),
        ]
        + [pltpu.SemaphoreType.DMA((ring,))] * 2
        + [pltpu.SemaphoreType.DMA((experts,))] * 4,
        compiler_params=pltpu.CompilerParams(
            collective_id=0, has_side_effects=True, vmem_limit_bytes=48 * 1024 * 1024
        ),
        cost_estimate=pl.CostEstimate(
            flops=6 * 1024 * 1024 * 1024, bytes_accessed=64 * 1024 * 1024, transcendentals=0
        ),
    )(
        all_rows,
        weight_share,
        jnp.pad(residual[0], ((0, 0), (0, extra))),
        moe_gain[None, :],
        w_gate[0],
        w_up[0],
        w_down[0],
        send_pick,
        first_pick,
        second_pick,
        route_weights[0],
    )
    return layer_out[None]


def solution(mesh):
    in_specs = (
        P("grp", "seq", None),
        P(),
        P("grp", "seq", None),
        P(),
        P(),
        P("grp", "seq", None),
        P(),
        P("grp", None),
        P("grp", "seq", None),
        P(),
        P("grp", None, None),
        P("grp", None, None),
        P("grp", None, None),
        P("grp", "seq", None),
        P("grp", "seq", None),
    )
    out_specs = P("grp", "seq", None)
    return jax.shard_map(
        on_device, mesh=mesh, in_specs=in_specs, out_specs=out_specs, check_vma=False
    )
```

```python
import functools

import jax
import jax.numpy as jnp
from jax import lax
from jax.experimental import pallas as pl
from jax.experimental.pallas import tpu as pltpu
from jax.sharding import PartitionSpec as P

EPSILON = 1e-05


def from_behind(value, axis, steps):
    count = lax.axis_size(axis)
    first, last = (max(0, -steps), min(count, count - steps))
    return lax.ppermute(value, axis, [(source, source + steps) for source in range(first, last)])


def mixer_kernel(
    chips,
    state_ref,
    reach_ref,
    c_ref,
    base_ref,
    fade_ref,
    gate_ref,
    gain_ref,
    rows_ref,
    gated,
    states,
    near_state_send,
    far_state_send,
    state_recv,
    near_rows_send,
    far_rows_send,
    rows_recv,
):
    me = lax.axis_index("seq")
    chip, core = me // 2, me % 2
    twin = chip * 2 + 1 - core
    half = jnp.bfloat16
    full = jnp.float32

    def far(step):
        return lax.rem(chip + step, chips) * 2 + core

    barrier = pltpu.get_barrier_semaphore()

    def greet(device):
        pl.semaphore_signal(
            barrier, inc=1, device_id={"seq": device}, device_id_type=pl.DeviceIdType.MESH
        )

    greet(twin)
    for step in range(1, chips):
        greet(far(step))
    pl.semaphore_wait(barrier, chips)

    def copy(slots, near_send, far_send, recv, step, near):
        return pltpu.make_async_remote_copy(
            src_ref=slots.at[2 * step] if near else slots.at[0],
            dst_ref=slots.at[2 * step + 1] if near else slots.at[2 * step],
            send_sem=near_send.at[step] if near else far_send.at[step],
            recv_sem=recv.at[2 * step + 1] if near else recv.at[2 * step],
            device_id={"seq": twin if near else far(step)},
            device_id_type=pl.DeviceIdType.MESH,
        )

    def exchange(*parts):
        for step in range(1, chips):
            copy(*parts, step, False).start()
        copy(*parts, 0, True).start()
        for step in range(1, chips):
            copy(*parts, step, False).wait_recv()
            copy(*parts, step, True).start()
        for step in range(chips):
            copy(*parts, step, True).wait_recv()

    def drain(*parts):
        for step in range(1, chips):
            copy(*parts, step, False).wait_send()
        for step in range(chips):
            copy(*parts, step, True).wait_send()

    state_parts = (states, near_state_send, far_state_send, state_recv)
    rows_parts = (rows_ref, near_rows_send, far_rows_send, rows_recv)
    states[0] = state_ref[...]
    exchange(*state_parts)
    width = gate_ref.shape[1]
    stretch = 512 if width % 512 == 0 else 128
    squares = jnp.zeros((gate_ref.shape[0], 1), full)
    for start in range(0, width, stretch):
        columns = slice(start, start + stretch)
        entering = jnp.zeros((states.shape[1], stretch), full)
        for slot in range(1, 2 * chips):
            entering = entering + reach_ref[slot : slot + 1, columns] * states[
                slot, :, columns
            ].astype(full)
        carried = jnp.dot(c_ref[...], entering.astype(half), preferred_element_type=full)
        gate = gate_ref[:, columns].astype(full)
        value = (base_ref[:, columns] + carried * fade_ref[:, columns]) * (
            gate * jax.nn.sigmoid(gate)
        )
        gated[:, columns] = value
        squares = squares + jnp.sum(value * value, axis=1, keepdims=True)
    scale = lax.rsqrt(squares * (1.0 / width) + EPSILON)
    for start in range(0, width, stretch):
        columns = slice(start, start + stretch)
        rows_ref[0, :, columns] = (gated[:, columns] * scale * gain_ref[:, columns]).astype(half)
    exchange(*rows_parts)
    drain(*state_parts)
    drain(*rows_parts)


def exchange_kernel(
    ring,
    experts,
    rows_hbm,
    weight_hbm,
    residual_hbm,
    gain_ref,
    gate_hbm,
    up_hbm,
    down_hbm,
    send_pick_ref,
    first_pick_ref,
    second_pick_ref,
    pair_ref,
    out_ref,
    weight_ref,
    rows_ref,
    residual_ref,
    gate_ref,
    up_ref,
    down_ref,
    share_out,
    share_in,
    mixed_ref,
    moe_ref,
    outgoing,
    arrived,
    result,
    returned,
    local_sem,
    share_send,
    share_recv,
    out_send,
    out_recv,
    back_send,
    back_recv,
):
    me = lax.axis_index("seq")
    mine = lax.axis_index("grp")
    width = moe_ref.shape[1]
    stretch = 512 if width % 512 == 0 else 128
    share = weight_ref.shape[1]
    capacity = outgoing.shape[1]
    half = jnp.bfloat16
    full = jnp.float32

    locals_ = [
        pltpu.make_async_copy(source, target, local_sem.at[index])
        for index, (source, target) in enumerate(
            (
                (weight_hbm, weight_ref),
                (rows_hbm, rows_ref),
                (residual_hbm, residual_ref),
                (gate_hbm, gate_ref),
                (up_hbm, up_ref),
                (down_hbm, down_ref),
            )
        )
    ]
    for copy in locals_:
        copy.start()

    barrier = pltpu.get_barrier_semaphore()

    def greet(axis, own, count):
        def step(shift, carry):
            pl.semaphore_signal(
                barrier,
                inc=1,
                device_id={axis: lax.rem(own + shift, count)},
                device_id_type=pl.DeviceIdType.MESH,
            )
            return carry

        lax.fori_loop(1, count, step, 0)

    greet("seq", me, ring)
    greet("grp", mine, experts)
    pl.semaphore_wait(barrier, ring - 1 + experts - 1)

    def source(slot):
        chips = ring // 2
        chip = lax.rem(me // 2 + chips - slot // 2, chips)
        return chip * 2 + lax.rem(me + slot, 2)

    def share_copy(slot):
        return pltpu.make_async_remote_copy(
            src_ref=share_out.at[slot],
            dst_ref=share_in.at[me],
            send_sem=share_send.at[slot],
            recv_sem=share_recv.at[me],
            device_id={"seq": source(slot)},
            device_id_type=pl.DeviceIdType.MESH,
        )

    def share_arrival(column):
        return pltpu.make_async_remote_copy(
            src_ref=share_out.at[0],
            dst_ref=share_in.at[column],
            send_sem=share_send.at[0],
            recv_sem=share_recv.at[column],
            device_id={"seq": source(1)},
            device_id_type=pl.DeviceIdType.MESH,
        )

    def out_copy(target, slot):
        return pltpu.make_async_remote_copy(
            src_ref=outgoing.at[target],
            dst_ref=arrived.at[slot],
            send_sem=out_send.at[target],
            recv_sem=out_recv.at[slot],
            device_id={"grp": target},
            device_id_type=pl.DeviceIdType.MESH,
        )

    def back_copy(target, slot):
        return pltpu.make_async_remote_copy(
            src_ref=result.at[target],
            dst_ref=returned.at[slot],
            send_sem=back_send.at[target],
            recv_sem=back_recv.at[slot],
            device_id={"grp": target},
            device_id_type=pl.DeviceIdType.MESH,
        )

    pairs = experts // 2
    other = lax.rem(mine + 1, experts)

    def partner(step):
        here = mine // 2
        if pairs & (pairs - 1):
            return lax.rem(here + step, pairs)
        place = 0
        bit = 1
        while bit < pairs:
            place = place + lax.rem(here // bit + step // bit, 2) * bit
            bit *= 2
        return place

    locals_[0].wait()
    locals_[1].wait()

    def project(index, carry):
        slot = ring - 1 - index
        share_out[slot] = jnp.dot(
            rows_ref[slot], weight_ref[...], preferred_element_type=full
        ).astype(half)

        @pl.when(slot > 0)
        def _():
            share_copy(slot).start()

        return carry

    lax.fori_loop(0, ring, project, 0)
    share_in[me] = share_out[0]
    locals_[2].wait()

    def mix(index, squares):
        @pl.when(index != me)
        def _():
            share_arrival(index).wait_recv()

        column = pl.multiple_of(index * share, share)
        values = (
            residual_ref[:, pl.ds(column, share)].astype(full) + share_in[index].astype(full)
        ).astype(half)
        mixed_ref[:, pl.ds(column, share)] = values
        wide = values.astype(full)
        return squares + jnp.sum(wide * wide, axis=1, keepdims=True)

    squares = lax.fori_loop(0, ring, mix, jnp.zeros((mixed_ref.shape[0], 1), full))
    scale = lax.rsqrt(squares * (1.0 / width) + EPSILON)
    moe_ref[...] = (mixed_ref[:, :width].astype(full) * scale * gain_ref[...]).astype(half)

    def dispatch(index, carry):
        low = partner(pairs - 1 - index) * 2
        outgoing[pl.ds(low, 2)] = (
            jnp.dot(
                send_pick_ref[pl.ds(low, 2)].reshape(2 * capacity, moe_ref.shape[0]),
                moe_ref[...],
                preferred_element_type=full,
            )
            .astype(half)
            .reshape(2, capacity, width)
        )
        for target in (low, low + 1):

            @pl.when(target != mine)
            def _():
                out_copy(target, mine).start()

        return carry

    lax.fori_loop(0, pairs, dispatch, 0)
    arrived[mine] = outgoing[mine]
    for copy in locals_[3:]:
        copy.wait()

    def run_expert(step, carry):
        low = partner(step) * 2
        for origin in (low, low + 1):

            @pl.when(origin != mine)
            def _():
                out_copy(other, origin).wait_recv()

        rows = arrived[pl.ds(low, 2)].reshape(2 * capacity, width)
        gate_part = jnp.dot(rows, gate_ref[...], preferred_element_type=full)
        up_part = jnp.dot(rows, up_ref[...], preferred_element_type=full)
        hidden = (gate_part * jax.nn.sigmoid(gate_part) * up_part).astype(half)
        made = jnp.dot(hidden, down_ref[...], preferred_element_type=full).astype(half)
        result[pl.ds(low, 2)] = made.reshape(2, capacity, width)
        for origin in (low, low + 1):

            @pl.when(origin != mine)
            def _():
                back_copy(origin, mine).start()

        return carry

    lax.fori_loop(0, pairs, run_expert, 0)
    returned[mine] = result[mine]

    def take_back(slot, carry):
        @pl.when(slot != mine)
        def _():
            back_copy(other, slot).wait_recv()

        return carry

    lax.fori_loop(0, experts, take_back, 0)
    first_weight = pair_ref[:, 0:1]
    second_weight = pair_ref[:, 1:2]

    def combine(tile, carry):
        column = pl.multiple_of(tile * stretch, stretch)
        rows = returned[:, :, pl.ds(column, stretch)].reshape(experts * capacity, stretch)
        first = jnp.dot(first_pick_ref[...], rows, preferred_element_type=full)
        second = jnp.dot(second_pick_ref[...], rows, preferred_element_type=full)
        out_ref[:, pl.ds(column, stretch)] = (
            mixed_ref[:, pl.ds(column, stretch)].astype(full)
            + first_weight * first
            + second_weight * second
        ).astype(half)
        return carry

    lax.fori_loop(0, width // stretch, combine, 0)

    def drain_seq(shift, carry):
        share_copy(shift).wait_send()
        return carry

    def drain_grp(target, carry):
        @pl.when(target != mine)
        def _():
            out_copy(target, mine).wait_send()
            back_copy(target, mine).wait_send()

        return carry

    lax.fori_loop(1, ring, drain_seq, 0)
    lax.fori_loop(0, experts, drain_grp, 0)


def on_device(
    conv_input,
    conv_weight,
    step_raw,
    rate_log,
    skip_gain,
    gate_input,
    norm_gain,
    out_weight,
    residual,
    moe_gain,
    w_gate,
    w_up,
    w_down,
    routes,
    route_weights,
):
    half = jnp.bfloat16
    ring = lax.axis_size("seq")
    own = lax.axis_index("seq")
    share = -(-out_weight.shape[1] // (ring * 128)) * 128
    extra = ring * share - out_weight.shape[1]
    weight_part = lax.dynamic_slice_in_dim(
        jnp.pad(out_weight, ((0, 0), (0, extra))), own * share, share, axis=1
    )
    weight_part, conv_input = lax.optimization_barrier((weight_part, conv_input))
    weight_share = lax.all_gather(weight_part, "grp", axis=0, tiled=True)
    frames_in = conv_input[0]
    row_count = frames_in.shape[0]
    tap_count = conv_weight.shape[0]
    channel_count = conv_weight.shape[1]
    head_count = rate_log.shape[0]
    inner_width = gate_input.shape[2]
    head_width = inner_width // head_count
    state_width = (channel_count - inner_width) // 2
    model_width = residual.shape[2]
    edge_rows = frames_in[row_count - (tap_count - 1) :]
    before = from_behind(edge_rows, "seq", 1)
    padded = jnp.concatenate([before, frames_in], axis=0).astype(jnp.float32)
    summed = conv_weight[0][None, :] * padded[0:row_count]
    for offset in range(1, tap_count):
        summed = summed + conv_weight[offset][None, :] * padded[offset : offset + row_count]
    signal = jax.nn.silu(summed).astype(jnp.bfloat16)
    x_part = signal[:, :inner_width]
    b_part = signal[:, inner_width : inner_width + state_width]
    c_part = signal[:, inner_width + state_width :]
    step_size = jax.nn.softplus(step_raw[0])
    log_decay = -step_size * jnp.exp(rate_log)[None, :]
    cumulative = jnp.cumsum(log_decay, axis=0)
    x_float = x_part.astype(jnp.float32)
    scores = jnp.dot(c_part, b_part.T, preferred_element_type=jnp.float32)
    positions = jnp.arange(row_count)
    causal = positions[:, None] >= positions[None, :]
    by_head = cumulative.T
    gap_log = by_head[:, :, None] - by_head[:, None, :]
    decay_mask = jnp.where(causal[None], jnp.exp(jnp.where(causal[None], gap_log, 0.0)), 0.0)
    mixing = (scores[None] * decay_mask * step_size.T[:, None, :]).astype(half)
    x_heads = x_part.reshape(row_count, head_count, head_width)
    tail_weight = jnp.exp(cumulative[-1][None, :] - cumulative) * step_size
    local_state = lax.dot_general(
        b_part,
        (x_float * jnp.repeat(tail_weight, head_width, axis=1)).astype(half),
        (((0,), (0,)), ((), ())),
        preferred_element_type=jnp.float32,
    ).astype(half)
    totals = lax.all_gather(cumulative[-1], "seq", axis=0)
    slot_ids = jnp.arange(ring)
    origin = (own // 2 - slot_ids // 2 + ring // 2) % (ring // 2) * 2 + (own + slot_ids) % 2
    between = (slot_ids[None, :] > origin[:, None]) & (slot_ids[None, :] < own)
    passed = jnp.sum(jnp.where(between[:, :, None], totals[None], 0.0), axis=1)
    reach = jnp.where((origin < own)[:, None], jnp.exp(passed), 0.0)
    within = jnp.einsum("hts,shp->thp", mixing, x_heads, preferred_element_type=jnp.float32)
    base = within.reshape(row_count, inner_width) + jnp.repeat(skip_gain, head_width)[None, :] * x_float
    vmem = pl.BlockSpec(memory_space=pltpu.VMEM)
    all_rows = pl.pallas_call(
        functools.partial(mixer_kernel, ring // 2),
        out_shape=jax.ShapeDtypeStruct((ring, row_count, inner_width), half),
        in_specs=[vmem] * 7,
        out_specs=vmem,
        scratch_shapes=[
            pltpu.VMEM((row_count, inner_width), jnp.float32),
            pltpu.VMEM((ring, state_width, inner_width), half),
        ]
        + [
            pltpu.SemaphoreType.DMA((ring // 2,)),
            pltpu.SemaphoreType.DMA((ring // 2,)),
            pltpu.SemaphoreType.DMA((ring,)),
        ]
        * 2,
        compiler_params=pltpu.CompilerParams(
            collective_id=1, has_side_effects=True, vmem_limit_bytes=32 * 1024 * 1024
        ),
        cost_estimate=pl.CostEstimate(
            flops=1024 * 1024 * 1024, bytes_accessed=64 * 1024 * 1024, transcendentals=0
        ),
    )(
        local_state,
        jnp.repeat(reach, head_width, axis=1),
        c_part,
        base,
        jnp.repeat(jnp.exp(cumulative), head_width, axis=1),
        gate_input[0],
        norm_gain[None, :],
    )
    experts = lax.axis_size("grp")
    capacity = 4 * row_count // experts
    flat_picks = routes[0].reshape(-1)
    member = (flat_picks[:, None] == jnp.arange(experts)[None, :]).astype(jnp.int32)
    position = jnp.cumsum(member, axis=0) - member
    slot_index = jnp.sum(position * member, axis=1)
    target = (flat_picks * capacity + slot_index).reshape(row_count, 2)
    slots = jnp.arange(experts * capacity)
    send_pick = (
        jnp.any(target[None, :, :] == slots[:, None, None], axis=2)
        .astype(half)
        .reshape(experts, capacity, row_count)
    )
    first_pick = (target[:, 0:1] == slots[None, :]).astype(half)
    second_pick = (target[:, 1:2] == slots[None, :]).astype(half)
    hidden_width = w_gate.shape[2]
    anywhere = pl.BlockSpec(memory_space=pl.ANY)
    slab = pltpu.VMEM((experts, capacity, model_width), half)
    piece = pltpu.VMEM((ring, row_count, share), half)
    whole_rows = pltpu.VMEM((row_count, model_width), half)
    layer_out = pl.pallas_call(
        functools.partial(exchange_kernel, ring, experts),
        out_shape=jax.ShapeDtypeStruct((row_count, model_width), half),
        in_specs=[anywhere, anywhere, anywhere, vmem, anywhere, anywhere, anywhere, vmem, vmem, vmem, vmem],
        out_specs=vmem,
        scratch_shapes=[
            pltpu.VMEM((inner_width, share), half),
            pltpu.VMEM((ring, row_count, inner_width), half),
            pltpu.VMEM((row_count, ring * share), half),
            pltpu.VMEM((model_width, hidden_width), half),
            pltpu.VMEM((model_width, hidden_width), half),
            pltpu.VMEM((hidden_width, model_width), half),
            piece,
            piece,
            pltpu.VMEM((row_count, ring * share), half),
            whole_rows,
            slab,
            slab,
            slab,
            slab,
            pltpu.SemaphoreType.DMA((6,)),
        ]
        + [pltpu.SemaphoreType.DMA((ring,))] * 2
        + [pltpu.SemaphoreType.DMA((experts,))] * 4,
        compiler_params=pltpu.CompilerParams(
            collective_id=0, has_side_effects=True, vmem_limit_bytes=48 * 1024 * 1024
        ),
        cost_estimate=pl.CostEstimate(
            flops=6 * 1024 * 1024 * 1024, bytes_accessed=64 * 1024 * 1024, transcendentals=0
        ),
    )(
        all_rows,
        weight_share,
        jnp.pad(residual[0], ((0, 0), (0, extra))),
        moe_gain[None, :],
        w_gate[0],
        w_up[0],
        w_down[0],
        send_pick,
        first_pick,
        second_pick,
        route_weights[0],
    )
    return layer_out[None]


def solution(mesh):
    in_specs = (
        P("grp", "seq", None),
        P(),
        P("grp", "seq", None),
        P(),
        P(),
        P("grp", "seq", None),
        P(),
        P("grp", None),
        P("grp", "seq", None),
        P(),
        P("grp", None, None),
        P("grp", None, None),
        P("grp", None, None),
        P("grp", "seq", None),
        P("grp", "seq", None),
    )
    out_specs = P("grp", "seq", None)
    return jax.shard_map(
        on_device, mesh=mesh, in_specs=in_specs, out_specs=out_specs, check_vma=False
    )
```

```python
import functools

import jax
import jax.numpy as jnp
from jax import lax
from jax.experimental import pallas as pl
from jax.experimental.pallas import tpu as pltpu
from jax.sharding import PartitionSpec as P

EPSILON = 1e-05


def from_behind(value, axis, steps):
    count = lax.axis_size(axis)
    first, last = (max(0, -steps), min(count, count - steps))
    return lax.ppermute(value, axis, [(source, source + steps) for source in range(first, last)])


def mixer_kernel(
    chips,
    state_ref,
    reach_ref,
    c_ref,
    base_ref,
    fade_ref,
    gate_ref,
    gain_ref,
    rows_ref,
    gated,
    states,
    near_state_send,
    far_state_send,
    state_recv,
    near_rows_send,
    far_rows_send,
    rows_recv,
):
    me = lax.axis_index("seq")
    chip, core = me // 2, me % 2
    twin = chip * 2 + 1 - core
    half = jnp.bfloat16
    full = jnp.float32

    def far(step):
        return lax.rem(chip + step, chips) * 2 + core

    barrier = pltpu.get_barrier_semaphore()

    def greet(device):
        pl.semaphore_signal(
            barrier, inc=1, device_id={"seq": device}, device_id_type=pl.DeviceIdType.MESH
        )

    greet(twin)
    for step in range(1, chips):
        greet(far(step))
    pl.semaphore_wait(barrier, chips)

    def copy(slots, near_send, far_send, recv, step, near):
        return pltpu.make_async_remote_copy(
            src_ref=slots.at[2 * step] if near else slots.at[0],
            dst_ref=slots.at[2 * step + 1] if near else slots.at[2 * step],
            send_sem=near_send.at[step] if near else far_send.at[step],
            recv_sem=recv.at[2 * step + 1] if near else recv.at[2 * step],
            device_id={"seq": twin if near else far(step)},
            device_id_type=pl.DeviceIdType.MESH,
        )

    def exchange(*parts):
        for step in range(1, chips):
            copy(*parts, step, False).start()
        copy(*parts, 0, True).start()
        for step in range(1, chips):
            copy(*parts, step, False).wait_recv()
            copy(*parts, step, True).start()
        for step in range(chips):
            copy(*parts, step, True).wait_recv()

    def drain(*parts):
        for step in range(1, chips):
            copy(*parts, step, False).wait_send()
        for step in range(chips):
            copy(*parts, step, True).wait_send()

    state_parts = (states, near_state_send, far_state_send, state_recv)
    rows_parts = (rows_ref, near_rows_send, far_rows_send, rows_recv)
    states[0] = state_ref[...]
    exchange(*state_parts)
    width = gate_ref.shape[1]
    stretch = 512 if width % 512 == 0 else 128
    squares = jnp.zeros((gate_ref.shape[0], 1), full)
    for start in range(0, width, stretch):
        columns = slice(start, start + stretch)
        entering = jnp.zeros((states.shape[1], stretch), full)
        for slot in range(1, 2 * chips):
            entering = entering + reach_ref[slot : slot + 1, columns] * states[
                slot, :, columns
            ].astype(full)
        carried = jnp.dot(c_ref[...], entering.astype(half), preferred_element_type=full)
        gate = gate_ref[:, columns].astype(full)
        value = (base_ref[:, columns] + carried * fade_ref[:, columns]) * (
            gate * jax.nn.sigmoid(gate)
        )
        gated[:, columns] = value
        squares = squares + jnp.sum(value * value, axis=1, keepdims=True)
    scale = lax.rsqrt(squares * (1.0 / width) + EPSILON)
    for start in range(0, width, stretch):
        columns = slice(start, start + stretch)
        rows_ref[0, :, columns] = (gated[:, columns] * scale * gain_ref[:, columns]).astype(half)
    exchange(*rows_parts)
    drain(*state_parts)
    drain(*rows_parts)


def exchange_kernel(
    ring,
    experts,
    rows_hbm,
    weight_hbm,
    residual_hbm,
    gain_ref,
    gate_hbm,
    up_hbm,
    down_hbm,
    send_pick_ref,
    first_pick_ref,
    second_pick_ref,
    pair_ref,
    out_ref,
    weight_ref,
    rows_ref,
    residual_ref,
    gate_ref,
    up_ref,
    down_ref,
    share_out,
    share_in,
    mixed_ref,
    moe_ref,
    outgoing,
    arrived,
    result,
    returned,
    hub_rows,
    hub_pick,
    hub_send,
    hub_recv,
    local_sem,
    share_send,
    share_recv,
    out_send,
    out_recv,
    back_send,
    back_recv,
):
    me = lax.axis_index("seq")
    mine = lax.axis_index("grp")
    width = moe_ref.shape[1]
    stretch = 512 if width % 512 == 0 else 128
    share = weight_ref.shape[1]
    capacity = outgoing.shape[1]
    half = jnp.bfloat16
    full = jnp.float32

    locals_ = [
        pltpu.make_async_copy(source, target, local_sem.at[index])
        for index, (source, target) in enumerate(
            (
                (weight_hbm, weight_ref),
                (rows_hbm, rows_ref),
                (residual_hbm, residual_ref),
                (gate_hbm, gate_ref),
                (up_hbm, up_ref),
                (down_hbm, down_ref),
            )
        )
    ]
    for copy in locals_:
        copy.start()

    barrier = pltpu.get_barrier_semaphore()

    def greet(axis, own, count):
        def step(shift, carry):
            pl.semaphore_signal(
                barrier,
                inc=1,
                device_id={axis: lax.rem(own + shift, count)},
                device_id_type=pl.DeviceIdType.MESH,
            )
            return carry

        lax.fori_loop(1, count, step, 0)

    greet("seq", me, ring)
    greet("grp", mine, experts)
    pl.semaphore_wait(barrier, ring - 1 + experts - 1)

    def source(slot):
        chips = ring // 2
        chip = lax.rem(me // 2 + chips - slot // 2, chips)
        return chip * 2 + lax.rem(me + slot, 2)

    def share_copy(slot):
        return pltpu.make_async_remote_copy(
            src_ref=share_out.at[slot],
            dst_ref=share_in.at[me],
            send_sem=share_send.at[slot],
            recv_sem=share_recv.at[me],
            device_id={"seq": source(slot)},
            device_id_type=pl.DeviceIdType.MESH,
        )

    def share_arrival(column):
        return pltpu.make_async_remote_copy(
            src_ref=share_out.at[0],
            dst_ref=share_in.at[column],
            send_sem=share_send.at[0],
            recv_sem=share_recv.at[column],
            device_id={"seq": source(1)},
            device_id_type=pl.DeviceIdType.MESH,
        )

    side = experts // 2
    hub = lax.rem(mine + side, experts)

    def out_copy(buffer, target, slot):
        return pltpu.make_async_remote_copy(
            src_ref=outgoing.at[buffer],
            dst_ref=arrived.at[slot],
            send_sem=out_send.at[buffer],
            recv_sem=out_recv.at[slot],
            device_id={"grp": target},
            device_id_type=pl.DeviceIdType.MESH,
        )

    hub_copies = [
        pltpu.make_async_remote_copy(
            src_ref=source_ref,
            dst_ref=target_ref,
            send_sem=hub_send.at[index],
            recv_sem=hub_recv.at[index],
            device_id={"grp": hub},
            device_id_type=pl.DeviceIdType.MESH,
        )
        for index, (source_ref, target_ref) in enumerate(
            (
                (moe_ref, hub_rows),
                (send_pick_ref.at[pl.ds(hub // side * side, side)], hub_pick),
            )
        )
    ]

    def back_copy(target, slot):
        return pltpu.make_async_remote_copy(
            src_ref=result.at[target],
            dst_ref=returned.at[slot],
            send_sem=back_send.at[target],
            recv_sem=back_recv.at[slot],
            device_id={"grp": target},
            device_id_type=pl.DeviceIdType.MESH,
        )

    pairs = experts // 2
    other = lax.rem(mine + 1, experts)

    def partner(step):
        here = mine // 2
        if pairs & (pairs - 1):
            return lax.rem(here + step, pairs)
        place = 0
        bit = 1
        while bit < pairs:
            place = place + lax.rem(here // bit + step // bit, 2) * bit
            bit *= 2
        return place

    locals_[0].wait()
    locals_[1].wait()

    def project(index, carry):
        slot = ring - 1 - index
        share_out[slot] = jnp.dot(
            rows_ref[slot], weight_ref[...], preferred_element_type=full
        ).astype(half)

        @pl.when(slot > 0)
        def _():
            share_copy(slot).start()

        return carry

    lax.fori_loop(0, ring, project, 0)
    share_in[me] = share_out[0]
    locals_[2].wait()

    def mix(index, squares):
        @pl.when(index != me)
        def _():
            share_arrival(index).wait_recv()

        column = pl.multiple_of(index * share, share)
        values = (
            residual_ref[:, pl.ds(column, share)].astype(full) + share_in[index].astype(full)
        ).astype(half)
        mixed_ref[:, pl.ds(column, share)] = values
        wide = values.astype(full)
        return squares + jnp.sum(wide * wide, axis=1, keepdims=True)

    squares = lax.fori_loop(0, ring, mix, jnp.zeros((mixed_ref.shape[0], 1), full))
    scale = lax.rsqrt(squares * (1.0 / width) + EPSILON)
    moe_ref[...] = (mixed_ref[:, :width].astype(full) * scale * gain_ref[...]).astype(half)

    for copy in hub_copies:
        copy.start()

    def fill(low, picks, rows):
        outgoing[pl.ds(low, 2)] = (
            jnp.dot(
                picks.reshape(2 * capacity, moe_ref.shape[0]), rows, preferred_element_type=full
            )
            .astype(half)
            .reshape(2, capacity, width)
        )

    def dispatch(index, carry):
        low = partner(pairs // 2 - 1 - index) * 2
        fill(low, send_pick_ref[pl.ds(low, 2)], moe_ref[...])
        for target in (low, low + 1):

            @pl.when(target != mine)
            def _():
                out_copy(target, target, mine).start()

        return carry

    def forward(index, carry):
        low = partner(pairs // 2 - 1 - index) * 2
        buffer = lax.rem(low + side, experts)
        fill(buffer, hub_pick[pl.ds(lax.rem(low, side), 2)], hub_rows[...])
        for turn in range(2):

            @pl.when(low + turn != mine)
            def _():
                out_copy(buffer + turn, low + turn, hub).start()

        return carry

    lax.fori_loop(0, pairs // 2, dispatch, 0)
    arrived[mine] = outgoing[mine]
    for copy in hub_copies:
        copy.wait_recv()
    lax.fori_loop(0, pairs // 2, forward, 0)
    arrived[hub] = outgoing[hub]
    for copy in locals_[3:]:
        copy.wait()

    def run_expert(step, carry):
        low = partner(step) * 2
        for origin in (low, low + 1):

            @pl.when((origin != mine) & (origin != hub))
            def _():
                out_copy(other, other, origin).wait_recv()

        rows = arrived[pl.ds(low, 2)].reshape(2 * capacity, width)
        gate_part = jnp.dot(rows, gate_ref[...], preferred_element_type=full)
        up_part = jnp.dot(rows, up_ref[...], preferred_element_type=full)
        hidden = (gate_part * jax.nn.sigmoid(gate_part) * up_part).astype(half)
        made = jnp.dot(hidden, down_ref[...], preferred_element_type=full).astype(half)
        result[pl.ds(low, 2)] = made.reshape(2, capacity, width)
        for origin in (low, low + 1):

            @pl.when(origin != mine)
            def _():
                back_copy(origin, mine).start()

        return carry

    lax.fori_loop(0, pairs, run_expert, 0)
    returned[mine] = result[mine]

    def take_back(slot, carry):
        @pl.when(slot != mine)
        def _():
            back_copy(other, slot).wait_recv()

        return carry

    lax.fori_loop(0, experts, take_back, 0)
    first_weight = pair_ref[:, 0:1]
    second_weight = pair_ref[:, 1:2]

    def combine(tile, carry):
        column = pl.multiple_of(tile * stretch, stretch)
        rows = returned[:, :, pl.ds(column, stretch)].reshape(experts * capacity, stretch)
        first = jnp.dot(first_pick_ref[...], rows, preferred_element_type=full)
        second = jnp.dot(second_pick_ref[...], rows, preferred_element_type=full)
        out_ref[:, pl.ds(column, stretch)] = (
            mixed_ref[:, pl.ds(column, stretch)].astype(full)
            + first_weight * first
            + second_weight * second
        ).astype(half)
        return carry

    lax.fori_loop(0, width // stretch, combine, 0)

    def drain_seq(shift, carry):
        share_copy(shift).wait_send()
        return carry

    def drain_grp(target, carry):
        @pl.when(target != mine)
        def _():
            back_copy(target, mine).wait_send()

        @pl.when((target != mine) & (target != hub))
        def _():
            out_copy(target, other, mine).wait_send()

        return carry

    lax.fori_loop(1, ring, drain_seq, 0)
    lax.fori_loop(0, experts, drain_grp, 0)
    for copy in hub_copies:
        copy.wait_send()


def on_device(
    conv_input,
    conv_weight,
    step_raw,
    rate_log,
    skip_gain,
    gate_input,
    norm_gain,
    out_weight,
    residual,
    moe_gain,
    w_gate,
    w_up,
    w_down,
    routes,
    route_weights,
):
    half = jnp.bfloat16
    ring = lax.axis_size("seq")
    own = lax.axis_index("seq")
    share = -(-out_weight.shape[1] // (ring * 128)) * 128
    extra = ring * share - out_weight.shape[1]
    weight_part = lax.dynamic_slice_in_dim(
        jnp.pad(out_weight, ((0, 0), (0, extra))), own * share, share, axis=1
    )
    weight_part, conv_input = lax.optimization_barrier((weight_part, conv_input))
    weight_share = lax.all_gather(weight_part, "grp", axis=0, tiled=True)
    frames_in = conv_input[0]
    row_count = frames_in.shape[0]
    tap_count = conv_weight.shape[0]
    channel_count = conv_weight.shape[1]
    head_count = rate_log.shape[0]
    inner_width = gate_input.shape[2]
    head_width = inner_width // head_count
    state_width = (channel_count - inner_width) // 2
    model_width = residual.shape[2]
    edge_rows = frames_in[row_count - (tap_count - 1) :]
    before = from_behind(edge_rows, "seq", 1)
    padded = jnp.concatenate([before, frames_in], axis=0).astype(jnp.float32)
    summed = conv_weight[0][None, :] * padded[0:row_count]
    for offset in range(1, tap_count):
        summed = summed + conv_weight[offset][None, :] * padded[offset : offset + row_count]
    signal = jax.nn.silu(summed).astype(jnp.bfloat16)
    x_part = signal[:, :inner_width]
    b_part = signal[:, inner_width : inner_width + state_width]
    c_part = signal[:, inner_width + state_width :]
    step_size = jax.nn.softplus(step_raw[0])
    log_decay = -step_size * jnp.exp(rate_log)[None, :]
    cumulative = jnp.cumsum(log_decay, axis=0)
    x_float = x_part.astype(jnp.float32)
    scores = jnp.dot(c_part, b_part.T, preferred_element_type=jnp.float32)
    positions = jnp.arange(row_count)
    causal = positions[:, None] >= positions[None, :]
    by_head = cumulative.T
    gap_log = by_head[:, :, None] - by_head[:, None, :]
    decay_mask = jnp.where(causal[None], jnp.exp(jnp.where(causal[None], gap_log, 0.0)), 0.0)
    mixing = (scores[None] * decay_mask * step_size.T[:, None, :]).astype(half)
    x_heads = x_part.reshape(row_count, head_count, head_width)
    tail_weight = jnp.exp(cumulative[-1][None, :] - cumulative) * step_size
    local_state = lax.dot_general(
        b_part,
        (x_float * jnp.repeat(tail_weight, head_width, axis=1)).astype(half),
        (((0,), (0,)), ((), ())),
        preferred_element_type=jnp.float32,
    ).astype(half)
    totals = lax.all_gather(cumulative[-1], "seq", axis=0)
    slot_ids = jnp.arange(ring)
    origin = (own // 2 - slot_ids // 2 + ring // 2) % (ring // 2) * 2 + (own + slot_ids) % 2
    between = (slot_ids[None, :] > origin[:, None]) & (slot_ids[None, :] < own)
    passed = jnp.sum(jnp.where(between[:, :, None], totals[None], 0.0), axis=1)
    reach = jnp.where((origin < own)[:, None], jnp.exp(passed), 0.0)
    within = jnp.einsum("hts,shp->thp", mixing, x_heads, preferred_element_type=jnp.float32)
    base = within.reshape(row_count, inner_width) + jnp.repeat(skip_gain, head_width)[None, :] * x_float
    vmem = pl.BlockSpec(memory_space=pltpu.VMEM)
    all_rows = pl.pallas_call(
        functools.partial(mixer_kernel, ring // 2),
        out_shape=jax.ShapeDtypeStruct((ring, row_count, inner_width), half),
        in_specs=[vmem] * 7,
        out_specs=vmem,
        scratch_shapes=[
            pltpu.VMEM((row_count, inner_width), jnp.float32),
            pltpu.VMEM((ring, state_width, inner_width), half),
        ]
        + [
            pltpu.SemaphoreType.DMA((ring // 2,)),
            pltpu.SemaphoreType.DMA((ring // 2,)),
            pltpu.SemaphoreType.DMA((ring,)),
        ]
        * 2,
        compiler_params=pltpu.CompilerParams(
            collective_id=1, has_side_effects=True, vmem_limit_bytes=32 * 1024 * 1024
        ),
        cost_estimate=pl.CostEstimate(
            flops=1024 * 1024 * 1024, bytes_accessed=64 * 1024 * 1024, transcendentals=0
        ),
    )(
        local_state,
        jnp.repeat(reach, head_width, axis=1),
        c_part,
        base,
        jnp.repeat(jnp.exp(cumulative), head_width, axis=1),
        gate_input[0],
        norm_gain[None, :],
    )
    experts = lax.axis_size("grp")
    capacity = 4 * row_count // experts
    flat_picks = routes[0].reshape(-1)
    member = (flat_picks[:, None] == jnp.arange(experts)[None, :]).astype(jnp.int32)
    position = jnp.cumsum(member, axis=0) - member
    slot_index = jnp.sum(position * member, axis=1)
    target = (flat_picks * capacity + slot_index).reshape(row_count, 2)
    slots = jnp.arange(experts * capacity)
    send_pick = (
        jnp.any(target[None, :, :] == slots[:, None, None], axis=2)
        .astype(half)
        .reshape(experts, capacity, row_count)
    )
    first_pick = (target[:, 0:1] == slots[None, :]).astype(half)
    second_pick = (target[:, 1:2] == slots[None, :]).astype(half)
    hidden_width = w_gate.shape[2]
    anywhere = pl.BlockSpec(memory_space=pl.ANY)
    slab = pltpu.VMEM((experts, capacity, model_width), half)
    piece = pltpu.VMEM((ring, row_count, share), half)
    whole_rows = pltpu.VMEM((row_count, model_width), half)
    layer_out = pl.pallas_call(
        functools.partial(exchange_kernel, ring, experts),
        out_shape=jax.ShapeDtypeStruct((row_count, model_width), half),
        in_specs=[anywhere, anywhere, anywhere, vmem, anywhere, anywhere, anywhere, vmem, vmem, vmem, vmem],
        out_specs=vmem,
        scratch_shapes=[
            pltpu.VMEM((inner_width, share), half),
            pltpu.VMEM((ring, row_count, inner_width), half),
            pltpu.VMEM((row_count, ring * share), half),
            pltpu.VMEM((model_width, hidden_width), half),
            pltpu.VMEM((model_width, hidden_width), half),
            pltpu.VMEM((hidden_width, model_width), half),
            piece,
            piece,
            pltpu.VMEM((row_count, ring * share), half),
            whole_rows,
            slab,
            slab,
            slab,
            slab,
            whole_rows,
            pltpu.VMEM((experts // 2, capacity, row_count), half),
            pltpu.SemaphoreType.DMA((2,)),
            pltpu.SemaphoreType.DMA((2,)),
            pltpu.SemaphoreType.DMA((6,)),
        ]
        + [pltpu.SemaphoreType.DMA((ring,))] * 2
        + [pltpu.SemaphoreType.DMA((experts,))] * 4,
        compiler_params=pltpu.CompilerParams(
            collective_id=0, has_side_effects=True, vmem_limit_bytes=48 * 1024 * 1024
        ),
        cost_estimate=pl.CostEstimate(
            flops=6 * 1024 * 1024 * 1024, bytes_accessed=64 * 1024 * 1024, transcendentals=0
        ),
    )(
        all_rows,
        weight_share,
        jnp.pad(residual[0], ((0, 0), (0, extra))),
        moe_gain[None, :],
        w_gate[0],
        w_up[0],
        w_down[0],
        send_pick,
        first_pick,
        second_pick,
        route_weights[0],
    )
    return layer_out[None]


def solution(mesh):
    in_specs = (
        P("grp", "seq", None),
        P(),
        P("grp", "seq", None),
        P(),
        P(),
        P("grp", "seq", None),
        P(),
        P("grp", None),
        P("grp", "seq", None),
        P(),
        P("grp", None, None),
        P("grp", None, None),
        P("grp", None, None),
        P("grp", "seq", None),
        P("grp", "seq", None),
    )
    out_specs = P("grp", "seq", None)
    return jax.shard_map(
        on_device, mesh=mesh, in_specs=in_specs, out_specs=out_specs, check_vma=False
    )
```
